32 devices in a mesh: outer: 4 (over y, x), inner: 8 (over z, core).
Axes of the slice: x: 2, y: 2, z: 4, core: 2. Of those that a mesh axis runs over, the one named last changes fastest.
Arguments:
- query_rows: bfloat16 [8192, 64], P(('outer', 'inner')), may hold values from -40 to 40, as said below
- key_rows: bfloat16 [8192, 64], P(('outer', 'inner')), may hold values from -40 to 40, as said below
- value_rows: bfloat16 [8192, 512], P(('outer', 'inner')), may hold values from -9 to 9, as said below
Outputs:
- linear_out: bfloat16 [8192, 512], P(('outer', 'inner'))
- window_out: bfloat16 [8192, 512], P(('outer', 'inner'))
The draws below stay inside these ranges and needn't reach their ends.
Inputs may be any that keep to these rules, and one draw needn't show every extreme that they name: `query_rows`: real-valued queries of each head. `key_rows`: real-valued keys of each head. `value_rows`: real-valued values.
All inputs are finite; a program needn't handle non-finite values.
Results may differ from the reference program's by a relative error of at most 0.0015.
The reference program's roundings to bfloat16 on the way count: a program that leaves them out, or rounds other values in their place, can miss the bound.
Values may be sent and summed in bfloat16 or wider, within the bound.
A program may use at most 128 MiB of HBM per device.

```python
import math
import jax
import jax.numpy as jnp
from jax import lax

H = 4
DK = 16
DV = 128
WIN = 64
TOK_DEV = 256
F = 273
BLOCK = 256
TOKENS = 8192


def hot_pair(key):
    row_count = TOKENS
    base_query = jnp.clip(jax.random.normal(jax.random.fold_in(key, 11), (row_count, H * DK), jnp.float32), -6.0, 6.0)
    base_key = jnp.clip(jax.random.normal(jax.random.fold_in(key, 12), (row_count, H * DK), jnp.float32), -3.0, 3.0)
    position = jnp.arange(row_count)
    trend = 0.5 + 1.5 * position.astype(jnp.float32) / row_count
    shard_count = row_count // TOK_DEV
    shard_log = jax.random.uniform(jax.random.fold_in(key, 16), (shard_count, 1), jnp.float32, -1.25, 1.25)
    shard_scale = jnp.repeat(jnp.exp(shard_log), TOK_DEV, axis=0)
    base_key = base_key * trend[:, None] * shard_scale
    return (base_query, base_key)


def draw_query_rows(key, part):
    return hot_pair(key)[0].astype(jnp.bfloat16)


def draw_key_rows(key, part):
    return hot_pair(key)[1].astype(jnp.bfloat16)


def draw_value_rows(key, part):
    row_count = TOKENS
    width = H * DV
    noise = jnp.clip(jax.random.normal(jax.random.fold_in(key, 21), (row_count, width), jnp.float32), -6.0, 6.0)
    magnitude = jax.random.uniform(jax.random.fold_in(key, 22), (1, width), jnp.float32, 1.0, 2.0)
    sign_bits = jax.random.randint(jax.random.fold_in(key, 23), (1, width), 0, 2)
    channel_mean = magnitude * (2.0 * sign_bits.astype(jnp.float32) - 1.0)
    shard_count = row_count // TOK_DEV
    shard_shift = 0.5 * jax.random.normal(jax.random.fold_in(key, 24), (shard_count, width), jnp.float32)
    shard_shift = jnp.repeat(jnp.clip(shard_shift, -1.0, 1.0), TOK_DEV, axis=0)
    values = jnp.clip(noise + channel_mean + shard_shift, -9.0, 9.0)
    return values.astype(jnp.bfloat16)


def setup_inputs(seed: int = 0) -> dict:
    splits = jax.random.split(jax.random.key(seed), 4)
    return {
        "query_rows": draw_query_rows(jax.random.fold_in(splits[3], 71), 0),
        "key_rows": draw_key_rows(jax.random.fold_in(splits[3], 71), 0),
        "value_rows": draw_value_rows(jax.random.fold_in(splits[3], 71), 0),
    }


inv_root_two = 1.0 / math.sqrt(2.0)

def features(inputs):
    row_count = inputs.shape[0]
    scaled = inputs.astype(jnp.float32).reshape(row_count, H, DK) * 0.5
    squares = (scaled[:, :, :, None] * scaled[:, :, None, :]).reshape(row_count, H, DK * DK) * inv_root_two
    stacked = jnp.concatenate([jnp.ones((row_count, H, 1), jnp.float32), scaled, squares], axis=2)
    return jnp.transpose(stacked, (1, 2, 0)).astype(jnp.bfloat16)

def reference(query_rows, key_rows, value_rows):
    high = lax.Precision.HIGHEST
    blocks = TOKENS // BLOCK
    key_pad = jnp.concatenate([jnp.zeros((WIN, H * DK), jnp.bfloat16), key_rows], axis=0)
    value_pad = jnp.concatenate([jnp.zeros((WIN, H * DV), jnp.bfloat16), value_rows], axis=0)

    def step(carry, block_index):
        state_sum, norm_sum = carry
        first_row = (block_index * BLOCK).astype(jnp.int32)
        query_block = lax.dynamic_slice_in_dim(query_rows, first_row, BLOCK, 0)
        key_block = lax.dynamic_slice_in_dim(key_rows, first_row, BLOCK, 0)
        value_block = lax.dynamic_slice_in_dim(value_rows, first_row, BLOCK, 0)
        key_window = lax.dynamic_slice_in_dim(key_pad, first_row, BLOCK + WIN, 0)
        value_window = lax.dynamic_slice_in_dim(value_pad, first_row, BLOCK + WIN, 0)
        query_feats = features(query_block).astype(jnp.float32)
        key_feats = features(key_block).astype(jnp.float32)
        query_heads = query_block.astype(jnp.float32).reshape(BLOCK, H, DK)
        key_heads = key_block.astype(jnp.float32).reshape(BLOCK, H, DK)
        value_heads = value_block.astype(jnp.float32).reshape(BLOCK, H, DV)
        numerator = jnp.einsum('hft,hfv->thv', query_feats, state_sum, precision=high)
        denominator = jnp.einsum('hft,hf->th', query_feats, norm_sum, precision=high)
        scores = jnp.einsum('thd,shd->hts', query_heads, key_heads, precision=high) * 0.25
        causal = jnp.arange(BLOCK)[:, None] >= jnp.arange(BLOCK)[None, :]
        kernel = jnp.where(causal[None], 1.0 + scores + 0.5 * scores * scores, 0.0)
        kernel_low = kernel.astype(jnp.bfloat16).astype(jnp.float32)
        numerator = numerator + jnp.einsum('hts,shv->thv', kernel_low, value_heads, precision=high)
        denominator = denominator + lax.optimization_barrier(jnp.sum(kernel, axis=2)).T
        linear_part = (numerator / denominator[:, :, None]).reshape(BLOCK, H * DV).astype(jnp.bfloat16)
        key_wheads = key_window.astype(jnp.float32).reshape(BLOCK + WIN, H, DK)
        value_wheads = value_window.astype(jnp.float32).reshape(BLOCK + WIN, H, DV)
        wscores = jnp.einsum('thd,shd->hts', query_heads, key_wheads, precision=high) * 0.25
        offset = jnp.arange(BLOCK + WIN)[None, :] - WIN - jnp.arange(BLOCK)[:, None]
        inside = (offset <= 0) & (offset >= -WIN) & (first_row + jnp.arange(BLOCK + WIN)[None, :] - WIN >= 0)
        wscores = jnp.where(inside[None], wscores, -1e+30)
        row_max = lax.optimization_barrier(jnp.max(wscores, axis=2, keepdims=True))
        weights = jnp.exp(wscores - row_max)
        weights = weights / lax.optimization_barrier(jnp.sum(weights, axis=2, keepdims=True))
        weights_low = weights.astype(jnp.bfloat16).astype(jnp.float32)
        window_part = jnp.einsum('hts,shv->thv', weights_low, value_wheads, precision=high)
        window_part = window_part.reshape(BLOCK, H * DV).astype(jnp.bfloat16)
        state_sum = state_sum + jnp.einsum('hft,thv->hfv', key_feats, value_heads, precision=high)
        norm_sum = norm_sum + lax.optimization_barrier(jnp.sum(key_feats, axis=2))
        return ((state_sum, norm_sum), (linear_part, window_part))
    start_carry = (jnp.zeros((H, F, DV), jnp.float32), jnp.zeros((H, F), jnp.float32))
    final_carry, outputs = lax.scan(step, start_carry, jnp.arange(blocks, dtype=jnp.int32))
    linear_out = outputs[0].reshape(TOKENS, H * DV)
    window_out = outputs[1].reshape(TOKENS, H * DV)
    return (linear_out, window_out)
```

```python
import functools
import math

import jax
import jax.numpy as jnp
from jax import lax
from jax.experimental import pallas as pl
from jax.experimental.pallas import tpu as pltpu
from jax.sharding import PartitionSpec as P

H = 4
DK = 16
DV = 128
WIN = 64
HALF_PAIRS = DK // 2
TAIL = DK + DK * HALF_PAIRS + HALF_PAIRS
ROWS = TAIL + 8
WIRE = jnp.float32

MESH = pl.DeviceIdType.MESH
inv_root_two = 1.0 / math.sqrt(2.0)


def feature_rows(scaled):
    parts = [scaled, scaled * scaled * inv_root_two]
    for d in range(1, HALF_PAIRS):
        rolled = jnp.concatenate([scaled[d:], scaled[:d]], axis=0)
        parts.append(scaled * rolled * inv_root_two)
    parts.append(scaled[:HALF_PAIRS] * scaled[HALF_PAIRS:] * inv_root_two)
    row = lax.broadcasted_iota(jnp.int32, (8, scaled.shape[1]), 0)
    parts.append(jnp.where(row == 0, 1.0, 0.0))
    return jnp.concatenate(parts, axis=0)


def dot(a, b, dims=((1,), (0,))):
    return lax.dot_general(a, b, (dims, ((), ())), preferred_element_type=jnp.float32)


def kernel(
    groups,
    inner,
    q_ref,
    k_ref,
    v_ref,
    lin_ref,
    win_ref,
    kext,
    vhalo,
    own,
    mate,
    tot,
    cols,
    gsum,
    gin,
    ret,
    pre,
    feats,
    num,
    den,
    halo_send,
    halo_recv,
    pair_send,
    pair_recv,
    col_send,
    col_recv,
    out_send,
    out_recv,
    ret_send,
    ret_recv,
    fwd_send,
    fwd_recv,
):
    f32, bf16 = jnp.float32, jnp.bfloat16
    length = q_ref.shape[0]
    n = inner // 2
    piece = tot.shape[1]
    half_rows = H // 2 * ROWS
    o = lax.axis_index("outer")
    i = lax.axis_index("inner")
    c = lax.rem(i, 2)
    z = lax.div(i, 2)
    flat = o * inner + i
    total = groups * inner
    nxt = lax.rem(flat + 1, total)
    prv = lax.rem(flat + total - 1, total)
    after = (lax.div(nxt, inner), lax.rem(nxt, inner))
    before = (lax.div(prv, inner), lax.rem(prv, inner))
    partner = (o, i + 1 - 2 * c)

    def chip(r):
        return lax.rem(z + r, n)

    column = [(o, chip(r) * 2 + c) for r in range(1, n)]
    others = [(lax.rem(o + r, groups), i) for r in range(1, groups)]

    barrier = pltpu.get_barrier_semaphore()
    peers = [partner, *column, *others, after, before]
    for peer in peers:
        pl.semaphore_signal(barrier, inc=1, device_id=peer, device_id_type=MESH)

    def remote(src, dst, send, recv, peer):
        return pltpu.make_async_remote_copy(
            src_ref=src, dst_ref=dst, send_sem=send, recv_sem=recv,
            device_id=peer, device_id_type=MESH,
        )

    keys = k_ref[...]
    keys_t = (keys.astype(f32) * 0.5).T
    ones = jnp.ones((8, length), bf16)
    row = lax.broadcasted_iota(jnp.int32, (8, DV), 0)
    rest = ROWS - DV

    def state(h):
        phi = feature_rows(keys_t[h * DK : (h + 1) * DK]).astype(bf16)
        part = dot(phi, v_ref[:, h * DV : (h + 1) * DV])
        norm = dot(ones, phi, ((1,), (1,)))
        high = jnp.concatenate([norm[:, DV:], jnp.zeros((8, DV - rest), f32)], axis=1)
        tail = jnp.where(row == 0, part[TAIL:], jnp.where(row == 1, norm[:, :DV], jnp.where(row == 2, high, 0.0)))
        first = h % 2 * ROWS
        own[h // 2, first : first + TAIL] = part[:TAIL]
        own[h // 2, first + TAIL : first + ROWS] = tail

    if own.shape[1] > half_rows:
        own[:, half_rows:] = jnp.zeros((2, own.shape[1] - half_rows, DV), f32)
    pair = [remote(own.at[j], mate.at[j], pair_send.at[j], pair_recv.at[j], partner) for j in range(2)]
    state(0)
    state(1)
    pl.semaphore_wait(barrier, len(peers))
    pair[0].start()
    state(2)
    state(3)
    pair[1].start()
    halo = [
        remote(k_ref.at[pl.ds(length - WIN, WIN)], kext, halo_send.at[0], halo_recv.at[0], after),
        remote(v_ref.at[pl.ds(length - WIN, WIN)], vhalo, halo_send.at[1], halo_recv.at[1], after),
    ]
    for copy in halo:
        copy.start()

    queries = q_ref[...]
    lane_head = lax.div(lax.broadcasted_iota(jnp.int32, queries.shape, 1), DK)

    def head_queries(h):
        return jnp.where(lane_head == h, queries, jnp.zeros_like(queries))

    def query_features():
        queries_t = (queries.astype(f32) * 0.5).T
        for h in range(H):
            phi = feature_rows(queries_t[h * DK : (h + 1) * DK])
            twice = lax.broadcasted_iota(jnp.int32, phi.shape, 0)
            weight = jnp.where((twice >= 2 * DK) & (twice < TAIL), 2.0, 1.0)
            feats[h] = (phi.astype(bf16).astype(f32) * weight).astype(bf16)

    step = 128

    def inside_block(h):
        q_h = head_queries(h)
        for first in range(0, length, step):
            end = first + step
            s = dot(q_h[first:end], keys[:end], ((1,), (1,))) * 0.25
            t_at = first + lax.broadcasted_iota(jnp.int32, s.shape, 0)
            u_at = lax.broadcasted_iota(jnp.int32, s.shape, 1)
            kern = jnp.where(t_at >= u_at, 1.0 + s + 0.5 * s * s, 0.0)
            den[h, first:end] = jnp.sum(kern, axis=1, keepdims=True)
            num[h, first:end] = dot(kern.astype(bf16), v_ref[:end, h * DV : (h + 1) * DV])

    def window(h):
        q_h = head_queries(h)
        at = slice(h * DV, (h + 1) * DV)
        for first in range(0, length, WIN):
            if first == 0:
                k_w = jnp.concatenate([kext[...], keys[:WIN]], axis=0)
                v_w = jnp.concatenate([vhalo[:, at], v_ref[:WIN, at]], axis=0)
            else:
                k_w = keys[first - WIN : first + WIN]
                v_w = v_ref[first - WIN : first + WIN, at]
            s = dot(q_h[first : first + WIN], k_w, ((1,), (1,))) * 0.25
            t_at = lax.broadcasted_iota(jnp.int32, s.shape, 0)
            u_at = lax.broadcasted_iota(jnp.int32, s.shape, 1)
            seen = (u_at >= t_at) & (u_at <= t_at + WIN)
            if first == 0:
                seen = seen & ((u_at >= WIN) | (flat > 0))
            s = jnp.where(seen, s, -1e30)
            e = jnp.exp(s - jnp.max(s, axis=1, keepdims=True))
            w = e / jnp.sum(e, axis=1, keepdims=True)
            win_ref[first : first + WIN, at] = dot(w.astype(bf16), v_w).astype(bf16)

    query_features()

    mine = remote(own.at[c], mate.at[c], pair_send.at[c], pair_recv.at[c], partner)
    mine.wait_recv()
    sums = own[c] + mate[c]
    tot[...] = sums.reshape(n, piece, DV).astype(tot.dtype)
    col = [
        remote(tot.at[chip(r)], cols.at[z], col_send.at[r - 1], col_recv.at[r - 1], column[r - 1])
        for r in range(1, n)
    ]
    for copy in col:
        copy.start()
    cols[z] = tot[z]
    inside_block(0)
    inside_block(1)
    inside_block(2)
    inside_block(3)
    for copy in col:
        copy.wait_recv()
    run = jnp.zeros((piece, DV), f32)
    befores = []
    for t in range(n):
        befores.append(run)
        run = run + cols[t].astype(f32)
    gsum[...] = run
    out = [
        remote(gsum, gin.at[r - 1], out_send.at[r - 1], out_recv.at[r - 1], others[r - 1])
        for r in range(1, groups)
    ]
    for copy in out:
        copy.start()
    for copy in halo:
        copy.wait()
    window(0)
    window(1)
    groups_before = jnp.zeros((piece, DV), f32)
    for r, copy in enumerate(out, 1):
        copy.wait_recv()
        groups_before = groups_before + jnp.where(r <= o, gin[r - 1], 0.0)
    for t in range(n):
        ret[t] = (befores[t] + groups_before).astype(ret.dtype)
    back = [
        remote(ret.at[chip(r)], pre.at[c, z], ret_send.at[r - 1], ret_recv.at[r - 1], column[r - 1])
        for r in range(1, n)
    ]
    for copy in back:
        copy.start()
    pre[c, z] = ret[z]

    def forward(r):
        src = lax.rem(z + n - r, n)
        return remote(pre.at[c, src], pre.at[c, src], fwd_send.at[r], fwd_recv.at[r], partner)

    fwd = [forward(r) for r in range(n)]
    fwd[0].start()
    window(2)
    window(3)
    for r in range(1, n):
        back[r - 1].wait_recv()
        fwd[r].start()
    other = remote(own.at[1 - c], mate.at[1 - c], pair_send.at[1 - c], pair_recv.at[1 - c], partner)
    other.wait_recv()
    for copy in fwd:
        copy.wait_recv()

    for h in range(H):
        first = h % 2 * ROWS
        held = pre[h // 2].reshape(n * piece, DV)[first : first + ROWS].astype(f32)
        held = held + jnp.where(c == 1, mate[h // 2, first : first + ROWS], 0.0)
        high = held.astype(bf16)
        low = (held - high.astype(f32)).astype(bf16)
        phi = feats[h]
        both = dot(phi, jnp.concatenate([high, low], axis=1), ((0,), (0,)))
        norm = jnp.concatenate([held[TAIL + 1 : TAIL + 2], held[TAIL + 2 : TAIL + 3, :rest]], axis=1)
        norm_high = norm.astype(bf16).astype(f32)
        norm_rows = jnp.concatenate([norm_high, norm - norm_high, jnp.zeros((6, ROWS), f32)], axis=0)
        bottom = dot(phi, norm_rows.astype(bf16), ((0,), (1,)))
        bottom = den[h] + bottom[:, 0:1] + bottom[:, 1:2]
        top = num[h] + both[:, :DV] + both[:, DV:]
        lin_ref[:, h * DV : (h + 1) * DV] = (top / bottom).astype(bf16)

    for copy in (*pair, *col, *out, *back, *fwd):
        copy.wait_send()


def shards(groups, inner, query_rows, key_rows, value_rows):
    length, width = value_rows.shape
    n = inner // 2
    half_rows = H // 2 * ROWS
    piece = -(-half_rows // (16 * n)) * 16
    f32 = jnp.float32
    dma = pltpu.SemaphoreType.DMA
    out = jax.ShapeDtypeStruct((length, width), jnp.bfloat16)
    vmem = pl.BlockSpec(memory_space=pltpu.VMEM)
    return pl.pallas_call(
        functools.partial(kernel, groups, inner),
        out_shape=(out, out),
        in_specs=[vmem] * 3,
        out_specs=(vmem, vmem),
        scratch_shapes=[
            pltpu.VMEM((WIN, H * DK), jnp.bfloat16),
            pltpu.VMEM((WIN, width), jnp.bfloat16),
            pltpu.VMEM((2, n * piece, DV), f32),
            pltpu.VMEM((2, n * piece, DV), f32),
            pltpu.VMEM((n, piece, DV), WIRE),
            pltpu.VMEM((n, piece, DV), WIRE),
            pltpu.VMEM((piece, DV), f32),
            pltpu.VMEM((groups - 1, piece, DV), f32),
            pltpu.VMEM((n, piece, DV), WIRE),
            pltpu.VMEM((2, n, piece, DV), WIRE),
            pltpu.VMEM((H, ROWS, length), jnp.bfloat16),
            pltpu.VMEM((H, length, DV), f32),
            pltpu.VMEM((H, length, 1), f32),
            dma((2,)), dma((2,)),
            dma((2,)), dma((2,)),
            dma((n - 1,)), dma((n - 1,)),
            dma((groups - 1,)), dma((groups - 1,)),
            dma((n - 1,)), dma((n - 1,)),
            dma((n,)), dma((n,)),
        ],
        compiler_params=pltpu.CompilerParams(collective_id=0, has_side_effects=True),
    )(query_rows, key_rows, value_rows)


def solution(mesh):
    rows = P(("outer", "inner"), None)
    return jax.shard_map(
        functools.partial(shards, mesh.shape["outer"], mesh.shape["inner"]),
        mesh=mesh,
        in_specs=(rows, rows, rows),
        out_specs=(rows, rows),
        check_vma=False,
    )
```

```python
import functools
import math

import jax
import jax.numpy as jnp
from jax import lax
from jax.experimental import pallas as pl
from jax.experimental.pallas import tpu as pltpu
from jax.sharding import PartitionSpec as P

H = 4
DK = 16
DV = 128
WIN = 64
HALF_PAIRS = DK // 2
TAIL = DK + DK * HALF_PAIRS + HALF_PAIRS
ROWS = TAIL + 8
WIRE = jnp.float32

MESH = pl.DeviceIdType.MESH
inv_root_two = 1.0 / math.sqrt(2.0)


def feature_rows(scaled):
    parts = [scaled, scaled * scaled * inv_root_two]
    for d in range(1, HALF_PAIRS):
        rolled = jnp.concatenate([scaled[d:], scaled[:d]], axis=0)
        parts.append(scaled * rolled * inv_root_two)
    parts.append(scaled[:HALF_PAIRS] * scaled[HALF_PAIRS:] * inv_root_two)
    row = lax.broadcasted_iota(jnp.int32, (8, scaled.shape[1]), 0)
    parts.append(jnp.where(row == 0, 1.0, 0.0))
    return jnp.concatenate(parts, axis=0)


def dot(a, b, dims=((1,), (0,))):
    return lax.dot_general(a, b, (dims, ((), ())), preferred_element_type=jnp.float32)


def kernel(
    groups,
    inner,
    q_ref,
    k_ref,
    v_ref,
    lin_ref,
    win_ref,
    kext,
    vhalo,
    own,
    mate,
    tot,
    cols,
    gsum,
    gin,
    ret,
    pre,
    feats,
    num,
    den,
    halo_send,
    halo_recv,
    pair_send,
    pair_recv,
    col_send,
    col_recv,
    out_send,
    out_recv,
    ret_send,
    ret_recv,
    fwd_send,
    fwd_recv,
):
    f32, bf16 = jnp.float32, jnp.bfloat16
    length = q_ref.shape[1]
    n = inner // 2
    piece = tot.shape[1]
    half_rows = H // 2 * ROWS
    o = lax.axis_index("outer")
    i = lax.axis_index("inner")
    c = lax.rem(i, 2)
    z = lax.div(i, 2)
    flat = o * inner + i
    total = groups * inner
    nxt = lax.rem(flat + 1, total)
    prv = lax.rem(flat + total - 1, total)
    after = (lax.div(nxt, inner), lax.rem(nxt, inner))
    before = (lax.div(prv, inner), lax.rem(prv, inner))
    partner = (o, i + 1 - 2 * c)

    def chip(r):
        return lax.rem(z + r, n)

    column = [(o, chip(r) * 2 + c) for r in range(1, n)]
    others = [(lax.rem(o + r, groups), i) for r in range(1, groups)]

    barrier = pltpu.get_barrier_semaphore()
    peers = [partner, *column, *others, after, before]
    for peer in peers:
        pl.semaphore_signal(barrier, inc=1, device_id=peer, device_id_type=MESH)

    def remote(src, dst, send, recv, peer):
        return pltpu.make_async_remote_copy(
            src_ref=src, dst_ref=dst, send_sem=send, recv_sem=recv,
            device_id=peer, device_id_type=MESH,
        )

    keys_t = k_ref[...].astype(f32) * 0.5
    ones = jnp.ones((8, length), bf16)
    row = lax.broadcasted_iota(jnp.int32, (8, DV), 0)
    rest = ROWS - DV
    step = 2 * WIN

    def state(h):
        phi = feature_rows(keys_t[h * DK : (h + 1) * DK]).astype(bf16)
        part = dot(phi, v_ref[:, h * DV : (h + 1) * DV])
        norm = dot(ones, phi, ((1,), (1,)))
        high = jnp.concatenate([norm[:, DV:], jnp.zeros((8, DV - rest), f32)], axis=1)
        tail = jnp.where(row == 0, part[TAIL:], jnp.where(row == 1, norm[:, :DV], jnp.where(row == 2, high, 0.0)))
        first = h % 2 * ROWS
        own[h // 2, first : first + TAIL] = part[:TAIL]
        own[h // 2, first + TAIL : first + ROWS] = tail

    if own.shape[1] > half_rows:
        own[:, half_rows:] = jnp.zeros((2, own.shape[1] - half_rows, DV), f32)
    pair = [remote(own.at[j], mate.at[j], pair_send.at[j], pair_recv.at[j], partner) for j in range(2)]
    state(0)
    state(1)
    pl.semaphore_wait(barrier, len(peers))
    pair[0].start()
    state(2)
    state(3)
    pair[1].start()
    halo = [
        remote(k_ref.at[:, pl.ds(length - step, step)], kext, halo_send.at[0], halo_recv.at[0], after),
        remote(v_ref.at[pl.ds(length - WIN, WIN)], vhalo, halo_send.at[1], halo_recv.at[1], after),
    ]
    for copy in halo:
        copy.start()

    queries = q_ref[...].astype(f32).T.astype(bf16)
    keys = k_ref[...].astype(f32).T.astype(bf16)
    lane_head = lax.div(lax.broadcasted_iota(jnp.int32, queries.shape, 1), DK)

    def head_queries(h):
        return jnp.where(lane_head == h, queries, jnp.zeros_like(queries))

    def query_features():
        queries_t = q_ref[...].astype(f32) * 0.5
        for h in range(H):
            phi = feature_rows(queries_t[h * DK : (h + 1) * DK])
            twice = lax.broadcasted_iota(jnp.int32, phi.shape, 0)
            weight = jnp.where((twice >= 2 * DK) & (twice < TAIL), 2.0, 1.0)
            feats[h] = (phi.astype(bf16).astype(f32) * weight).astype(bf16)

    def inside_block(h):
        q_h = head_queries(h)
        for first in range(0, length, step):
            end = first + step
            s = dot(q_h[first:end], keys[:end], ((1,), (1,))) * 0.25
            t_at = first + lax.broadcasted_iota(jnp.int32, s.shape, 0)
            u_at = lax.broadcasted_iota(jnp.int32, s.shape, 1)
            kern = jnp.where(t_at >= u_at, 1.0 + s + 0.5 * s * s, 0.0)
            den[h, first:end] = jnp.sum(kern, axis=1, keepdims=True)
            num[h, first:end] = dot(kern.astype(bf16), v_ref[:end, h * DV : (h + 1) * DV])

    def window(h):
        q_h = head_queries(h)
        at = slice(h * DV, (h + 1) * DV)
        for first in range(0, length, WIN):
            if first == 0:
                k_w = jnp.concatenate([kext[...].astype(f32).T[step - WIN :].astype(bf16), keys[:WIN]], axis=0)
                v_w = jnp.concatenate([vhalo[:, at], v_ref[:WIN, at]], axis=0)
            else:
                k_w = keys[first - WIN : first + WIN]
                v_w = v_ref[first - WIN : first + WIN, at]
            s = dot(q_h[first : first + WIN], k_w, ((1,), (1,))) * 0.25
            t_at = lax.broadcasted_iota(jnp.int32, s.shape, 0)
            u_at = lax.broadcasted_iota(jnp.int32, s.shape, 1)
            seen = (u_at >= t_at) & (u_at <= t_at + WIN)
            if first == 0:
                seen = seen & ((u_at >= WIN) | (flat > 0))
            s = jnp.where(seen, s, -1e30)
            e = jnp.exp(s - jnp.max(s, axis=1, keepdims=True))
            w = e / jnp.sum(e, axis=1, keepdims=True)
            win_ref[first : first + WIN, at] = dot(w.astype(bf16), v_w).astype(bf16)

    query_features()

    mine = remote(own.at[c], mate.at[c], pair_send.at[c], pair_recv.at[c], partner)
    mine.wait_recv()
    sums = own[c] + mate[c]
    tot[...] = sums.reshape(n, piece, DV).astype(tot.dtype)
    col = [
        remote(tot.at[chip(r)], cols.at[z], col_send.at[r - 1], col_recv.at[r - 1], column[r - 1])
        for r in range(1, n)
    ]
    for copy in col:
        copy.start()
    cols[z] = tot[z]
    inside_block(0)
    inside_block(1)
    inside_block(2)
    inside_block(3)
    for copy in col:
        copy.wait_recv()
    run = jnp.zeros((piece, DV), f32)
    befores = []
    for t in range(n):
        befores.append(run)
        run = run + cols[t].astype(f32)
    gsum[...] = run
    out = [
        remote(gsum, gin.at[r - 1], out_send.at[r - 1], out_recv.at[r - 1], others[r - 1])
        for r in range(1, groups)
    ]
    for copy in out:
        copy.start()
    for copy in halo:
        copy.wait()
    window(0)
    window(1)
    groups_before = jnp.zeros((piece, DV), f32)
    for r, copy in enumerate(out, 1):
        copy.wait_recv()
        groups_before = groups_before + jnp.where(r <= o, gin[r - 1], 0.0)
    for t in range(n):
        ret[t] = (befores[t] + groups_before).astype(ret.dtype)
    back = [
        remote(ret.at[chip(r)], pre.at[c, z], ret_send.at[r - 1], ret_recv.at[r - 1], column[r - 1])
        for r in range(1, n)
    ]
    for copy in back:
        copy.start()
    pre[c, z] = ret[z]

    def forward(r):
        src = lax.rem(z + n - r, n)
        return remote(pre.at[c, src], pre.at[c, src], fwd_send.at[r], fwd_recv.at[r], partner)

    fwd = [forward(r) for r in range(n)]
    fwd[0].start()
    window(2)
    window(3)
    for r in range(1, n):
        back[r - 1].wait_recv()
        fwd[r].start()
    other = remote(own.at[1 - c], mate.at[1 - c], pair_send.at[1 - c], pair_recv.at[1 - c], partner)
    other.wait_recv()
    for copy in fwd:
        copy.wait_recv()

    for h in range(H):
        first = h % 2 * ROWS
        held = pre[h // 2].reshape(n * piece, DV)[first : first + ROWS].astype(f32)
        held = held + jnp.where(c == 1, mate[h // 2, first : first + ROWS], 0.0)
        high = held.astype(bf16)
        low = (held - high.astype(f32)).astype(bf16)
        phi = feats[h]
        both = dot(phi, jnp.concatenate([high, low], axis=1), ((0,), (0,)))
        norm = jnp.concatenate([held[TAIL + 1 : TAIL + 2], held[TAIL + 2 : TAIL + 3, :rest]], axis=1)
        norm_high = norm.astype(bf16).astype(f32)
        norm_rows = jnp.concatenate([norm_high, norm - norm_high, jnp.zeros((6, ROWS), f32)], axis=0)
        bottom = dot(phi, norm_rows.astype(bf16), ((0,), (1,)))
        bottom = den[h] + bottom[:, 0:1] + bottom[:, 1:2]
        top = num[h] + both[:, :DV] + both[:, DV:]
        lin_ref[:, h * DV : (h + 1) * DV] = (top / bottom).astype(bf16)

    for copy in (*pair, *col, *out, *back, *fwd):
        copy.wait_send()


def shards(groups, inner, query_rows, key_rows, value_rows):
    length, width = value_rows.shape
    n = inner // 2
    half_rows = H // 2 * ROWS
    piece = -(-half_rows // (16 * n)) * 16
    f32 = jnp.float32
    dma = pltpu.SemaphoreType.DMA
    out = pltpu.VMEM((length, width), jnp.bfloat16)
    vmem = pl.BlockSpec(memory_space=pltpu.VMEM)
    return pl.pallas_call(
        functools.partial(kernel, groups, inner),
        out_shape=(out, out),
        in_specs=[vmem] * 3,
        out_specs=(vmem, vmem),
        scratch_shapes=[
            pltpu.VMEM((H * DK, 2 * WIN), jnp.bfloat16),
            pltpu.VMEM((WIN, width), jnp.bfloat16),
            pltpu.VMEM((2, n * piece, DV), f32),
            pltpu.VMEM((2, n * piece, DV), f32),
            pltpu.VMEM((n, piece, DV), WIRE),
            pltpu.VMEM((n, piece, DV), WIRE),
            pltpu.VMEM((piece, DV), f32),
            pltpu.VMEM((groups - 1, piece, DV), f32),
            pltpu.VMEM((n, piece, DV), WIRE),
            pltpu.VMEM((2, n, piece, DV), WIRE),
            pltpu.VMEM((H, ROWS, length), jnp.bfloat16),
            pltpu.VMEM((H, length, DV), f32),
            pltpu.VMEM((H, length, 1), f32),
            dma((2,)), dma((2,)),
            dma((2,)), dma((2,)),
            dma((n - 1,)), dma((n - 1,)),
            dma((groups - 1,)), dma((groups - 1,)),
            dma((n - 1,)), dma((n - 1,)),
            dma((n,)), dma((n,)),
        ],
        compiler_params=pltpu.CompilerParams(collective_id=0, has_side_effects=True),
    )(query_rows.T, key_rows.T, value_rows)


def solution(mesh):
    rows = P(("outer", "inner"), None)
    return jax.shard_map(
        functools.partial(shards, mesh.shape["outer"], mesh.shape["inner"]),
        mesh=mesh,
        in_specs=(rows, rows, rows),
        out_specs=(rows, rows),
        check_vma=False,
    )
```

```python
import functools
import math

import jax
import jax.numpy as jnp
from jax import lax
from jax.experimental import pallas as pl
from jax.experimental.pallas import tpu as pltpu
from jax.sharding import PartitionSpec as P

H = 4
DK = 16
DV = 128
WIN = 64
HALF_PAIRS = DK // 2
TAIL = DK + DK * HALF_PAIRS + HALF_PAIRS
ROWS = TAIL + 8
WIRE = jnp.float32
SPLIT = 4

MESH = pl.DeviceIdType.MESH
inv_root_two = 1.0 / math.sqrt(2.0)


def feature_rows(scaled):
    parts = [scaled, scaled * scaled * inv_root_two]
    for d in range(1, HALF_PAIRS):
        rolled = jnp.concatenate([scaled[d:], scaled[:d]], axis=0)
        parts.append(scaled * rolled * inv_root_two)
    parts.append(scaled[:HALF_PAIRS] * scaled[HALF_PAIRS:] * inv_root_two)
    row = lax.broadcasted_iota(jnp.int32, (8, scaled.shape[1]), 0)
    parts.append(jnp.where(row == 0, 1.0, 0.0))
    return jnp.concatenate(parts, axis=0)


def dot(a, b, dims=((1,), (0,))):
    return lax.dot_general(a, b, (dims, ((), ())), preferred_element_type=jnp.float32)


def kernel(
    groups,
    inner,
    q_ref,
    k_ref,
    v_ref,
    lin_ref,
    win_ref,
    kext,
    vhalo,
    own,
    mate,
    tot,
    cols,
    gsum,
    gin,
    gsum_before,
    befores,
    ret,
    pre,
    feats,
    num,
    den,
    halo_send,
    halo_recv,
    pair_send,
    pair_recv,
    col_send,
    col_recv,
    out_send,
    out_recv,
    ret_send,
    ret_recv,
    fwd_send,
    fwd_recv,
    hello,
    go,
):
    f32, bf16 = jnp.float32, jnp.bfloat16
    length = q_ref.shape[1]
    n = inner // 2
    piece = tot.shape[1]
    half_rows = H // 2 * ROWS
    o = lax.axis_index("outer")
    i = lax.axis_index("inner")
    c = lax.rem(i, 2)
    z = lax.div(i, 2)
    flat = o * inner + i
    total = groups * inner
    nxt = lax.rem(flat + 1, total)
    after = (lax.div(nxt, inner), lax.rem(nxt, inner))
    partner = (o, i + 1 - 2 * c)

    def chip(r):
        return lax.rem(z + r, n)

    barrier = pltpu.get_barrier_semaphore()
    mates = [(o, chip(r) * 2 + 1) for r in range(1, n)]
    crowd = [(lax.rem(o + r, groups), z * 2 + 1) for r in range(1, groups)]
    chips = total // 2
    here = o * n + z
    ends = [lax.rem(here + 1, chips), lax.rem(here + chips - 1, chips)]
    peers = [*mates, *crowd, *[(lax.div(e, n), lax.rem(e, n) * 2 + 1) for e in ends]]

    @pl.when(c == 1)
    def _():
        pl.semaphore_signal(barrier, inc=1, device_id=partner, device_id_type=MESH)

    @pl.when(c == 0)
    def _():
        pl.semaphore_wait(barrier, 1)
        pl.semaphore_signal(hello, inc=1, device_id=partner, device_id_type=MESH)

    @pl.when(c == 1)
    def _():
        pl.semaphore_wait(hello, 1)
        for peer in peers:
            pl.semaphore_signal(barrier, inc=1, device_id=peer, device_id_type=MESH)

    def remote(src, dst, send, recv, peer):
        return pltpu.make_async_remote_copy(
            src_ref=src, dst_ref=dst, send_sem=send, recv_sem=recv,
            device_id=peer, device_id_type=MESH,
        )

    ones = jnp.ones((8, length), bf16)
    row = lax.broadcasted_iota(jnp.int32, (8, DV), 0)
    rest = ROWS - DV
    step = 2 * WIN

    def state(half, j):
        h = half * (H // 2) + j
        scaled = k_ref[pl.ds(pl.multiple_of(h * DK, DK), DK), :].astype(f32) * 0.5
        phi = feature_rows(scaled).astype(bf16)
        part = dot(phi, v_ref[:, pl.ds(pl.multiple_of(h * DV, DV), DV)])
        norm = dot(ones, phi, ((1,), (1,)))
        high = jnp.concatenate([norm[:, DV:], jnp.zeros((8, DV - rest), f32)], axis=1)
        tail = jnp.where(row == 0, part[TAIL:], jnp.where(row == 1, norm[:, :DV], jnp.where(row == 2, high, 0.0)))
        first = j * ROWS
        own[half, first : first + TAIL] = part[:TAIL]
        own[half, first + TAIL : first + ROWS] = tail

    if own.shape[1] > half_rows:
        own[:, half_rows:] = jnp.zeros((2, own.shape[1] - half_rows, DV), f32)
        mate[:, half_rows:] = jnp.zeros((2, own.shape[1] - half_rows, DV), f32)
    pair = []
    for j in range(H // 2):
        state(1 - c, j)
        at = pl.ds(j * ROWS, ROWS)
        pair.append(
            remote(own.at[1 - c, at], mate.at[1 - c, at], pair_send.at[j], pair_recv.at[j], partner)
        )
        pair[j].start()
    for j in range(H // 2):
        state(c, j)
    at = pl.ds(0, half_rows)
    spare = remote(own.at[0, at], mate.at[0, at], pair_send.at[H // 2], pair_recv.at[H // 2], partner)
    halo = [
        remote(k_ref.at[:, pl.ds(length - step, step)], kext, halo_send.at[0], halo_recv.at[0], after),
        remote(v_ref.at[pl.ds(length - WIN, WIN)], vhalo, halo_send.at[1], halo_recv.at[1], after),
    ]

    queries = q_ref[...].astype(f32).T.astype(bf16)
    keys = k_ref[...].astype(f32).T.astype(bf16)
    lane_head = lax.div(lax.broadcasted_iota(jnp.int32, queries.shape, 1), DK)

    def head_queries(h):
        return jnp.where(lane_head == h, queries, jnp.zeros_like(queries))

    def query_features():
        queries_t = q_ref[...].astype(f32) * 0.5
        for h in range(H):
            phi = feature_rows(queries_t[h * DK : (h + 1) * DK])
            twice = lax.broadcasted_iota(jnp.int32, phi.shape, 0)
            weight = jnp.where((twice >= 2 * DK) & (twice < TAIL), 2.0, 1.0)
            feats[h] = (phi.astype(bf16).astype(f32) * weight).astype(bf16)

    def inside_block(h):
        q_h = head_queries(h)
        for first in range(0, length, step):
            end = first + step
            s = dot(q_h[first:end], keys[:end], ((1,), (1,))) * 0.25
            t_at = first + lax.broadcasted_iota(jnp.int32, s.shape, 0)
            u_at = lax.broadcasted_iota(jnp.int32, s.shape, 1)
            kern = jnp.where(t_at >= u_at, 1.0 + s + 0.5 * s * s, 0.0)
            den[h, first:end] = jnp.sum(kern, axis=1, keepdims=True)
            num[h, first:end] = dot(kern.astype(bf16), v_ref[:end, h * DV : (h + 1) * DV])

    def window(h):
        q_h = head_queries(h)
        at = slice(h * DV, (h + 1) * DV)
        for first in range(0, length, WIN):
            if first == 0:
                k_w = jnp.concatenate([kext[...].astype(f32).T[step - WIN :].astype(bf16), keys[:WIN]], axis=0)
                v_w = jnp.concatenate([vhalo[:, at], v_ref[:WIN, at]], axis=0)
            else:
                k_w = keys[first - WIN : first + WIN]
                v_w = v_ref[first - WIN : first + WIN, at]
            s = dot(q_h[first : first + WIN], k_w, ((1,), (1,))) * 0.25
            t_at = lax.broadcasted_iota(jnp.int32, s.shape, 0)
            u_at = lax.broadcasted_iota(jnp.int32, s.shape, 1)
            seen = (u_at >= t_at) & (u_at <= t_at + WIN)
            if first == 0:
                seen = seen & ((u_at >= WIN) | (flat > 0))
            s = jnp.where(seen, s, -1e30)
            e = jnp.exp(s - jnp.max(s, axis=1, keepdims=True))
            w = e / jnp.sum(e, axis=1, keepdims=True)
            win_ref[first : first + WIN, at] = dot(w.astype(bf16), v_w).astype(bf16)

    query_features()

    @pl.when(c == 1)
    def _():
        pl.semaphore_wait(barrier, len(peers))
        pl.semaphore_signal(go, inc=1, device_id=partner, device_id_type=MESH)

    @pl.when(c == 0)
    def _():
        pl.semaphore_wait(go, 1)

    def column_copy(t):
        return remote(tot.at[t], cols.at[z], col_send.at[t], col_recv.at[z], (o, t * 2 + c))

    def column_arrival(t):
        return remote(tot.at[t], cols.at[t], col_send.at[t], col_recv.at[t], (o, t * 2 + c))

    def far_first(k):
        return jnp.where(z < n // 2, n - 1 - k, k)

    for j in range(H // 2):
        pair[j].wait_recv()
    tot[...] = (own[c] + mate[c]).reshape(n, piece, DV).astype(tot.dtype)
    for k in range(n):
        t = far_first(k)

        @pl.when(z != t)
        def _(t=t):
            column_copy(t).start()

    @pl.when(c == 0)
    def _():
        spare.start()

    for copy in halo:
        copy.start()
    cols[z] = tot[z]
    inside_block(0)
    inside_block(1)
    inside_block(2)
    inside_block(3)
    for t in range(n):
        @pl.when(z != t)
        def _(t=t):
            column_arrival(t).wait_recv()

    run = jnp.zeros((piece, DV), f32)
    for t in range(n):
        befores[t] = run
        run = run + cols[t].astype(f32)
    gsum[...] = run
    def group_copy(g, k):
        return remote(gsum, gin.at[o], out_send.at[k], out_recv.at[o], (g, i))

    later = []
    for r in range(1, groups):
        g = lax.rem(o + jnp.where(lax.rem(o, 2) == 0, groups - r, r), groups)
        later.append(g)

        @pl.when(g > o)
        def _(g=g, r=r):
            group_copy(g, r - 1).start()

    for copy in halo:
        copy.wait()
    window(0)
    gsum_before[...] = jnp.zeros((piece, DV), f32)
    for g in range(groups - 1):
        @pl.when(g < o)
        def _(g=g):
            remote(gsum, gin.at[g], out_send.at[0], out_recv.at[g], (g, i)).wait_recv()
            gsum_before[...] += gin[g]

    groups_before = gsum_before[...]

    def back_copy(t):
        return remote(ret.at[t], pre.at[c, z], ret_send.at[t], ret_recv.at[z], (o, t * 2 + c))

    def back_arrival(t):
        return remote(ret.at[t], pre.at[c, t], ret_send.at[t], ret_recv.at[t], (o, t * 2 + c))

    for k in range(n):
        t = far_first(k)
        ret[t] = (befores[t] + groups_before).astype(ret.dtype)

        @pl.when(z != t)
        def _(t=t):
            back_copy(t).start()

    pre[c, z] = ret[z]

    def forward(t):
        return remote(pre.at[c, t], pre.at[c, t], fwd_send.at[t], fwd_recv.at[t], partner)

    def forward_arrival(t):
        return remote(pre.at[1 - c, t], pre.at[1 - c, t], fwd_send.at[t], fwd_recv.at[t], partner)

    forward(z).start()
    window(1)
    window(2)
    window(3)
    for d in range(1, n):
        for t in (z - d, z + d):
            @pl.when((t >= 0) & (t < n))
            def _(t=t):
                back_arrival(t).wait_recv()
                forward(t).start()

    @pl.when(c == 1)
    def _():
        spare.wait_recv()

    for t in range(n):
        forward_arrival(t).wait_recv()

    for h in range(H):
        first = h % 2 * ROWS
        held = pre[h // 2].reshape(n * piece, DV)[first : first + ROWS].astype(f32)
        held = held + jnp.where(c == 1, mate[h // 2, first : first + ROWS], 0.0)
        high = held.astype(bf16)
        low = (held - high.astype(f32)).astype(bf16)
        phi = feats[h]
        both = dot(phi, jnp.concatenate([high, low], axis=1), ((0,), (0,)))
        norm = jnp.concatenate([held[TAIL + 1 : TAIL + 2], held[TAIL + 2 : TAIL + 3, :rest]], axis=1)
        norm_high = norm.astype(bf16).astype(f32)
        norm_rows = jnp.concatenate([norm_high, norm - norm_high, jnp.zeros((6, ROWS), f32)], axis=0)
        bottom = dot(phi, norm_rows.astype(bf16), ((0,), (1,)))
        bottom = den[h] + bottom[:, 0:1] + bottom[:, 1:2]
        top = num[h] + both[:, :DV] + both[:, DV:]
        lin_ref[:, h * DV : (h + 1) * DV] = (top / bottom).astype(bf16)

    @pl.when(c == 0)
    def _():
        spare.wait_send()

    for t in range(n):
        @pl.when(z != t)
        def _(t=t):
            column_copy(t).wait_send()
            back_copy(t).wait_send()

        forward(t).wait_send()
    for k, g in enumerate(later):
        @pl.when(g > o)
        def _(g=g, k=k):
            group_copy(g, k).wait_send()

    for copy in pair:
        copy.wait_send()


def place(lin_vmem, win_vmem, lin_out, win_out, sems):
    rows = lin_vmem.shape[0] // SPLIT
    copies = []
    for a, (src, dst) in enumerate(((lin_vmem, lin_out), (win_vmem, win_out))):
        for b in range(SPLIT):
            at = pl.ds(b * rows, rows)
            copies.append(pltpu.make_async_copy(src.at[at], dst.at[at], sems.at[a, b]))
            copies[-1].start()
    for copy in copies:
        copy.wait()


def shards(groups, inner, query_rows, key_rows, value_rows):
    length, width = value_rows.shape
    n = inner // 2
    half_rows = H // 2 * ROWS
    piece = -(-half_rows // (16 * n)) * 16
    f32 = jnp.float32
    dma = pltpu.SemaphoreType.DMA
    out = pltpu.VMEM((length, width), jnp.bfloat16)
    vmem = pl.BlockSpec(memory_space=pltpu.VMEM)
    held = pl.pallas_call(
        functools.partial(kernel, groups, inner),
        out_shape=(out, out),
        in_specs=[vmem] * 3,
        out_specs=(vmem, vmem),
        scratch_shapes=[
            pltpu.VMEM((H * DK, 2 * WIN), jnp.bfloat16),
            pltpu.VMEM((WIN, width), jnp.bfloat16),
            pltpu.VMEM((2, n * piece, DV), f32),
            pltpu.VMEM((2, n * piece, DV), f32),
            pltpu.VMEM((n, piece, DV), WIRE),
            pltpu.VMEM((n, piece, DV), WIRE),
            pltpu.VMEM((piece, DV), f32),
            pltpu.VMEM((groups, piece, DV), f32),
            pltpu.VMEM((piece, DV), f32),
            pltpu.VMEM((n, piece, DV), f32),
            pltpu.VMEM((n, piece, DV), WIRE),
            pltpu.VMEM((2, n, piece, DV), WIRE),
            pltpu.VMEM((H, ROWS, length), jnp.bfloat16),
            pltpu.VMEM((H, length, DV), f32),
            pltpu.VMEM((H, length, 1), f32),
            dma((2,)), dma((2,)),
            dma((H // 2 + 1,)), dma((H // 2 + 1,)),
            dma((n,)), dma((n,)),
            dma((groups - 1,)), dma((groups,)),
            dma((n,)), dma((n,)),
            dma((n,)), dma((n,)),
            pltpu.SemaphoreType.REGULAR, pltpu.SemaphoreType.REGULAR,
        ],
        compiler_params=pltpu.CompilerParams(collective_id=0, has_side_effects=True),
    )(query_rows.T, key_rows.T, value_rows)
    hbm = pl.BlockSpec(memory_space=pl.ANY)
    placed = jax.ShapeDtypeStruct((length, width), jnp.bfloat16)
    return pl.pallas_call(
        place,
        out_shape=(placed, placed),
        in_specs=[vmem] * 2,
        out_specs=(hbm, hbm),
        scratch_shapes=[dma((2, SPLIT))],
    )(*[pltpu.with_memory_space_constraint(x, pltpu.VMEM) for x in held])


def solution(mesh):
    rows = P(("outer", "inner"), None)
    return jax.shard_map(
        functools.partial(shards, mesh.shape["outer"], mesh.shape["inner"]),
        mesh=mesh,
        in_specs=(rows, rows, rows),
        out_specs=(rows, rows),
        check_vma=False,
    )
```
